32 devices in a mesh: fault: 16 (over z, x, core), member: 2 (over y).
Axes of the slice: x: 2, y: 2, z: 4, core: 2. Of those that a mesh axis runs over, the one named last changes fastest.
Arguments:
- log_rate: float32 [8, 16384], P('member', 'fault'), may hold values from -2.5 to 2.5
- log_state: float32 [8, 16384], P('member', 'fault'), may hold values from -2.5 to 2.5
- direct_effect: float32 [8, 16384], P('member', 'fault'), may hold values from 0.01 to 0.03
- evolution_effect: float32 [8, 16384], P('member', 'fault'), may hold values from 0.01 to 0.04
- slip_distance: float32 [8, 16384], P('member', 'fault'), may hold values from 0.5 to 2
- normal_stress: float32 [16384], P('fault'), may hold values from 10 to 40
- near_blocks: bfloat16 [128, 24, 128, 128], P(('fault', 'member')), may hold values from -0.25 to 0.25
- near_columns: int32 [128, 24], P(('fault', 'member')), may hold values from 0 to 127, as said below
- near_count: int32 [128], P(('fault', 'member')), may hold values from 1 to 24, as said below
- far_clusters: int32 [128, 3], P(('fault', 'member')), may hold values from 0 to 3, as said below
- far_basis: bfloat16 [128, 3, 32, 128], P(('fault', 'member')), may hold values from -0.625 to 0.625
- column_basis: bfloat16 [32, 16384], P(None, ('fault', 'member')), may hold values from -0.09375 to 0.09375
Outputs:
- rate_next: float32 [8, 16384], P('member', 'fault')
- state_next: float32 [8, 16384], P('member', 'fault')
The draws below stay inside these ranges and needn't reach their ends.
Inputs may be any that keep to these rules, and one draw needn't show every extreme that they name: `near_columns`: slot 0 of row p holds p; the slots of a row hold distinct block indices, all among the 8 block rows of p's index of fault and of the indices before and after it, counted periodically. `near_count`: slots at or beyond the count are ignored; every row of at least one index of fault has all 24 slots live. `far_clusters`: the clusters of one row are distinct.
All inputs are finite; a program needn't handle non-finite values.
Results may differ from the reference program's by a relative error of at most 0.0019.
Values may be sent and summed in bfloat16 or wider, within the bound.
No kernel may reach another device: no remote copies, remote signals or barrier semaphores. Data moves between devices by JAX's collectives and lax.ppermute only.
A program may use at most 64 MiB of HBM per device.

```python
import math
import jax
import jax.numpy as jnp
from jax import lax

PANEL = 128
PDEV = 8
NEARMAX = 24
NFAR = 3
RANK = 32
GROUP = 4
NP = 128
NE = 16384
MEM = 8
NCLUS = 4


def draw_near_columns(key, part):
    width = 3 * PDEV
    rows = jnp.arange(NP, dtype=jnp.int32)
    device = rows // PDEV
    own_slot = PDEV + rows % PDEV
    scores = jax.random.randint(key, (NP, width), 0, 4096, dtype=jnp.int32) * width + jnp.arange(width, dtype=jnp.int32)[None, :]
    scores = jnp.where(jnp.arange(width, dtype=jnp.int32)[None, :] == own_slot[:, None], -1, scores)
    order = jnp.argsort(scores, axis=1, stable=True)[:, :NEARMAX].astype(jnp.int32)
    return ((device[:, None] - 1) * PDEV + order) % NP


def draw_near_count(key, part):
    first_key, second_key = jax.random.split(jax.random.fold_in(key, 17))
    device = jnp.arange(NP, dtype=jnp.int32) // PDEV
    chosen = jax.random.randint(first_key, (), 0, 8, dtype=jnp.int32)
    lower = jax.random.randint(second_key, (NP,), 1, 7, dtype=jnp.int32)
    return jnp.where(device % 8 == chosen, NEARMAX, lower).astype(jnp.int32)


def draw_far_clusters(key, part):
    scores = jax.random.randint(jax.random.fold_in(key, 29), (NP, NCLUS), 0, 4096, dtype=jnp.int32) * NCLUS + jnp.arange(NCLUS, dtype=jnp.int32)[None, :]
    return jnp.argsort(scores, axis=1, stable=True)[:, :NFAR].astype(jnp.int32)


def level_of(key, dims, pieces, smallest, high):
    def one(position, parts):
        heights = jax.random.uniform(jax.random.fold_in(jax.random.fold_in(key, 6), position), (parts,), jnp.float32, smallest / len(pieces), high / len(pieces))
        return jnp.repeat(jnp.exp(heights), dims[position] // parts).reshape((-1,) + (1,) * (len(dims) - position - 1))

    loudness = one(*pieces[0])
    for cut in pieces[1:]:
        loudness = loudness * one(*cut)
    return loudness


def scatter_about(key, shape, scale, limit, cuts=(), kind=jnp.bfloat16):
    values = jax.random.normal(key, shape, jnp.float32) * scale
    if len(cuts) > 0:
        values = level_of(key, shape, cuts, -0.22, 0.18) * values
    return jnp.clip(values, min=-limit, max=limit).astype(kind)


def setup_inputs(seed: int = 0) -> dict:
    streams_of = jax.random.split(jax.random.key(seed), 13)
    return {
        "log_rate": scatter_about(streams_of[0], (MEM, NE), 0.5, 2.5, ((0, 2), (1, 16)), jnp.float32),
        "log_state": scatter_about(streams_of[1], (MEM, NE), 0.5, 2.5, ((0, 2), (1, 16)), jnp.float32),
        "direct_effect": jnp.clip(jnp.exp(math.log(0.03) - 1.0986123 * jax.random.uniform(streams_of[2], (MEM, NE), jnp.float32) ** level_of(streams_of[2], (MEM, NE), ((0, 2), (1, 16)), -0.2, 0.2)), 0.01, 0.03),
        "evolution_effect": jnp.clip(jnp.exp(math.log(0.04) - 1.3862944 * jax.random.uniform(streams_of[3], (MEM, NE), jnp.float32) ** level_of(streams_of[3], (MEM, NE), ((0, 2), (1, 16)), -0.2, 0.2)), 0.01, 0.04),
        "slip_distance": jnp.clip(jnp.exp(math.log(2.0) - 1.3862944 * jax.random.uniform(streams_of[4], (MEM, NE), jnp.float32) ** level_of(streams_of[4], (MEM, NE), ((0, 2), (1, 16)), -0.2, 0.2)), 0.5, 2.0),
        "normal_stress": jnp.clip(10.0 + 30.0 * jax.random.uniform(streams_of[5], (NE,), jnp.float32) ** level_of(streams_of[5], (NE,), ((0, 16),), -0.2, 0.2), 10.0, 40.0),
        "near_blocks": scatter_about(streams_of[6], (NP, NEARMAX, PANEL, PANEL), (4 * PANEL) ** -0.5, 0.25, ((0, 32),)),
        "near_columns": draw_near_columns(jax.random.fold_in(streams_of[12], 71), 0),
        "near_count": draw_near_count(jax.random.fold_in(streams_of[12], 71), 0),
        "far_clusters": draw_far_clusters(jax.random.fold_in(streams_of[12], 71), 0),
        "far_basis": scatter_about(streams_of[10], (NP, NFAR, RANK, PANEL), (RANK * NFAR) ** -0.5, 0.625, ((0, 32),)),
        "column_basis": scatter_about(streams_of[11], (RANK, NE), (GROUP * PDEV * PANEL) ** -0.5, 0.09375, ((1, 32),)),
    }


damping = 0.5
time_step = 0.25


def reference(log_rate, log_state, direct_effect, evolution_effect, slip_distance, normal_stress, near_blocks, near_columns, near_count, far_clusters, far_basis, column_basis):
    members = log_rate.shape[0]
    velocity = jnp.exp(log_rate)
    deficit = (1.0 - velocity).astype(jnp.bfloat16)
    coeffs = jnp.einsum('qcx,mcx->cqm', column_basis.astype(jnp.float32).reshape(RANK, NCLUS, -1), deficit.astype(jnp.float32).reshape(members, NCLUS, -1), precision=lax.Precision.HIGHEST)
    coeff_rounded = coeffs.astype(jnp.bfloat16)
    panels = deficit.reshape(members, NP, PANEL)

    def one_row(row_items):
        blocks, columns, live_count, clusters_row, basis_row = row_items
        picked = panels[:, columns, :].astype(jnp.float32)
        active = jnp.arange(NEARMAX) < live_count
        picked = jnp.where(active[None, :, None], picked, 0.0)
        near_field = jnp.einsum('msj,sje->me', picked, blocks.astype(jnp.float32), precision=lax.Precision.HIGHEST)
        chosen = coeff_rounded[clusters_row].astype(jnp.float32)
        far_field = jnp.einsum('kqm,kqe->me', chosen, basis_row.astype(jnp.float32), precision=lax.Precision.HIGHEST)
        return near_field + far_field

    row_results = lax.map(one_row, (near_blocks, near_columns, near_count, far_clusters, far_basis))
    stress_rate = jnp.transpose(row_results, (1, 0, 2)).reshape(members, NP * PANEL)
    state_rate = (jnp.exp(-log_state) - velocity) / slip_distance
    rate_change = (stress_rate - normal_stress[None, :] * evolution_effect * state_rate) / (normal_stress[None, :] * direct_effect + damping * velocity)
    return log_rate + time_step * rate_change, log_state + time_step * state_rate
```

```python
import jax
import jax.numpy as jnp
from jax import lax
from jax.sharding import PartitionSpec as P

PANEL = 128
GROUP = 4


damping = 0.5
time_step = 0.25


def swapped(block, axis, partner):
    count = lax.axis_size(axis)
    return lax.ppermute(block, axis, [(i, partner(i) % count) for i in range(count)])


def per_device(
    log_rate,
    log_state,
    direct_effect,
    evolution_effect,
    slip_distance,
    normal_stress,
    near_blocks,
    near_columns,
    near_count,
    far_clusters,
    far_basis,
    column_basis,
):
    fault_count = lax.axis_size("fault")
    member_count = lax.axis_size("member")
    fault_pos = lax.axis_index("fault")
    member_pos = lax.axis_index("member")
    local_members, elements = log_rate.shape
    own_panels = elements // PANEL
    total_panels = own_panels * fault_count
    row_count, slots = near_columns.shape
    row_width = row_count * PANEL
    rank_size = column_basis.shape[0]
    cluster_total = fault_count // GROUP
    bf16, f32 = jnp.bfloat16, jnp.float32
    pair = member_count == 2

    def gathered(block):
        if pair:
            return jnp.stack([block, swapped(block, "member", lambda i: i ^ 1)])
        return lax.all_gather(block, "member", axis=0)

    def in_order(stacked):
        if pair:
            flip = member_pos == 1
            return jnp.where(flip, stacked[::-1], stacked)
        return stacked

    log_rate_all = gathered(log_rate)
    column_all = gathered(column_basis)
    far_by_cluster = jnp.zeros((row_count, cluster_total, rank_size, PANEL), bf16)
    for k in range(far_clusters.shape[1]):
        mine = far_clusters[:, k, None] == jnp.arange(cluster_total)[None, :]
        far_by_cluster = jnp.where(mine[:, :, None, None], far_basis[:, k, None], far_by_cluster)
    far_all = gathered(far_by_cluster.reshape(row_count, cluster_total * rank_size, PANEL))

    velocity = jnp.exp(log_rate)
    deficit = (1.0 - velocity).astype(bf16)
    deficit_all = (1.0 - jnp.exp(log_rate_all)).astype(bf16)
    members = member_count * local_members
    deficit_all = deficit_all.reshape(members, elements)
    columns = jnp.moveaxis(in_order(column_all), 0, 1).reshape(rank_size, elements)
    partial_value = lax.dot_general(
        deficit, columns, (((1,), (1,)), ((), ())), preferred_element_type=f32
    )

    near_side = swapped(deficit_all, "fault", lambda i: i ^ 1)
    total = partial_value + swapped(partial_value, "fault", lambda i: i ^ 1)
    far_side = swapped(deficit_all, "fault", lambda i: i + 1 if i % 2 else i - 1)
    bit = 2
    while bit < GROUP:
        total = total + swapped(total, "fault", lambda i: i ^ bit)
        bit *= 2
    table = total.astype(bf16)[None]
    while bit < fault_count:
        other = swapped(table, "fault", lambda i: i ^ bit)
        upper = (fault_pos // bit) % 2 == 1
        table = jnp.where(upper, jnp.concatenate([other, table]), jnp.concatenate([table, other]))
        bit *= 2

    offset = (near_columns - (fault_pos - 1) * own_panels) % total_panels
    side = offset // own_panels
    odd = fault_pos % 2
    place = jnp.where(side == 1, 0, jnp.where((side == 0) == (odd == 1), 1, 2))
    local_cols = place * own_panels + offset % own_panels
    window = jnp.concatenate([deficit_all, near_side, far_side], axis=1)
    panel_view = window.reshape(members, -1, PANEL)
    active = jnp.arange(slots)[None, :] < near_count[:, None]
    picked = panel_view[:, local_cols, :]
    picked = jnp.where(active[None, :, :, None], picked, jnp.zeros((), bf16))
    near_field = jnp.einsum("mrsj,rsje->mre", picked, near_blocks, preferred_element_type=f32)
    near_field = near_field.reshape(member_count, local_members, row_width)
    if pair:
        near_other = swapped(near_field[1], "member", lambda i: i ^ 1)
        near_rows = jnp.stack([near_field[0], near_other])
    else:
        near_rows = lax.all_to_all(near_field, "member", 0, 0)

    chosen = jnp.moveaxis(table, 1, 0).reshape(local_members, cluster_total * rank_size)
    far_rows = jnp.einsum("mk,hrke->hmre", chosen, far_all, preferred_element_type=f32)
    stress = near_rows + far_rows.reshape(member_count, local_members, row_width)
    stress = jnp.moveaxis(in_order(stress), 0, 1).reshape(local_members, elements)
    state_rate = (jnp.exp(-log_state) - velocity) / slip_distance
    rate_change = (stress - normal_stress[None, :] * evolution_effect * state_rate) / (
        normal_stress[None, :] * direct_effect + damping * velocity
    )
    return (log_rate + time_step * rate_change, log_state + time_step * state_rate)


def solution(mesh):
    return jax.shard_map(
        per_device,
        mesh=mesh,
        in_specs=(
            P("member", "fault"),
            P("member", "fault"),
            P("member", "fault"),
            P("member", "fault"),
            P("member", "fault"),
            P("fault"),
            P(("fault", "member"), None, None, None),
            P(("fault", "member"), None),
            P(("fault", "member")),
            P(("fault", "member"), None),
            P(("fault", "member"), None, None, None),
            P(None, ("fault", "member")),
        ),
        out_specs=(P("member", "fault"), P("member", "fault")),
        check_vma=False,
    )
```

```python
import functools

import jax
import jax.numpy as jnp
from jax import lax
from jax.experimental import pallas as pl
from jax.experimental.pallas import tpu as pltpu
from jax.sharding import PartitionSpec as P

PANEL = 128
GROUP = 4
COST = 10**9


damping = 0.5
time_step = 0.25

IN_SMEM = pl.BlockSpec(memory_space=pltpu.SMEM)
IN_VMEM = pl.BlockSpec(memory_space=pltpu.VMEM)
f32 = jnp.float32
bf16 = jnp.bfloat16


def swapped(block, axis, partner):
    count = lax.axis_size(axis)
    return lax.ppermute(block, axis, [(i, partner(i) % count) for i in range(count)])


def place_of(parts, pos, h):
    return pos ^ h if parts == 2 else h


def span(start, width):
    return pl.ds(pl.multiple_of(start, PANEL), width)


def deficit_kernel(rate_ref, out_ref):
    out_ref[...] = (1.0 - jnp.exp(rate_ref[...])).astype(bf16)


def partial_kernel(parts, pos_ref, deficit_ref, *refs):
    column_refs, out_ref = refs[:parts], refs[parts]
    total = None
    for h in range(parts):
        width = column_refs[h].shape[1]
        piece = lax.dot_general(
            deficit_ref[:, span(place_of(parts, pos_ref[0], h) * width, width)],
            column_refs[h][...],
            (((1,), (1,)), ((), ())),
            preferred_element_type=f32,
        )
        total = piece if total is None else total + piece
    out_ref[...] = total


def far_kernel(cluster_ref, own_cluster_ref, basis_ref, out_ref):
    rows, slots, rank, panel = basis_ref.shape
    clusters = out_ref.shape[0] // rank
    for r in range(rows):
        for j in range(clusters):
            wanted = own_cluster_ref[0] ^ j
            block = jnp.zeros((rank, panel), f32)
            for k in range(slots):
                live = cluster_ref[r, k] == wanted
                block = jnp.where(live, basis_ref[r, k].astype(f32), block)
            out_ref[j * rank : (j + 1) * rank, r * panel : (r + 1) * panel] = block.astype(bf16)


def near_kernel(own_panels, total_panels, column_ref, count_ref, pos_ref, own_ref, near_ref, far_ref, blocks_ref, out_ref, window, picked):
    rows, slots = column_ref.shape
    members = own_ref.shape[0]
    odd = pos_ref[0] % 2
    for side, start in ((own_ref, own_panels), (near_ref, (1 - odd) * 2 * own_panels), (far_ref, odd * 2 * own_panels)):
        for j in range(own_panels):
            window[start + j] = side[:, j * PANEL : (j + 1) * PANEL].astype(f32)
    window[3 * own_panels] = jnp.zeros((members, PANEL), f32)
    base = (pos_ref[0] - 1) * own_panels
    for r in range(rows):
        for s in range(slots):
            place = lax.rem(column_ref[r, s] - base + total_panels, total_panels)
            place = jnp.where(s < count_ref[r], place, 3 * own_panels)
            picked[r, :, s * PANEL : (s + 1) * PANEL] = window[place].astype(bf16)
        out_ref[:, r * PANEL : (r + 1) * PANEL] = jnp.dot(
            picked[r], blocks_ref[r].reshape(slots * PANEL, PANEL), preferred_element_type=f32
        )


def last_kernel(parts, pos_ref, low_ref, high_ref, *refs):
    far_refs, near_refs = refs[:parts], refs[parts : 2 * parts]
    base_ref, scale_ref, out_ref = refs[2 * parts :]
    depth = low_ref.shape[1]
    for h in range(parts):
        width = near_refs[h].shape[1]
        lanes = span(place_of(parts, pos_ref[0], h) * width, width)
        stress = (
            near_refs[h][...]
            + jnp.dot(low_ref[...], far_refs[h][:depth], preferred_element_type=f32)
            + jnp.dot(high_ref[...], far_refs[h][depth:], preferred_element_type=f32)
        )
        out_ref[:, lanes] = base_ref[:, lanes] + scale_ref[:, lanes] * stress


def per_device(
    log_rate,
    log_state,
    direct_effect,
    evolution_effect,
    slip_distance,
    normal_stress,
    near_blocks,
    near_columns,
    near_count,
    far_clusters,
    far_basis,
    column_basis,
):
    fault_count = lax.axis_size("fault")
    parts = lax.axis_size("member")
    fault_pos = lax.axis_index("fault")
    member_pos = lax.axis_index("member")
    local_members, elements = log_rate.shape
    own_panels = elements // PANEL
    total_panels = own_panels * fault_count
    row_count, slots = near_columns.shape
    row_width = row_count * PANEL
    rank_size = column_basis.shape[0]
    cluster_total = fault_count // GROUP
    members = parts * local_members
    def gathered(block):
        if parts == 2:
            return [block, swapped(block, "member", lambda i: i ^ 1)]
        every = lax.all_gather(block, "member", axis=0)
        return [every[h] for h in range(parts)]

    def call(body, name, out_shape, specs, mib=2, flops=10**6, scratch=()):
        return pl.pallas_call(
            body,
            out_shape=jax.ShapeDtypeStruct(*out_shape),
            in_specs=specs,
            out_specs=IN_VMEM,
            scratch_shapes=scratch,
            compiler_params=pltpu.CompilerParams(vmem_limit_bytes=mib << 20),
            cost_estimate=pl.CostEstimate(flops=flops, bytes_accessed=1, transcendentals=0),
            name=name,
        )

    columns = gathered(column_basis)
    deficit = call(deficit_kernel, "deficit", ((local_members, elements), bf16), [IN_VMEM], flops=COST)(log_rate)
    deficits = gathered(deficit)
    far_by_cluster = call(
        far_kernel, "far_by_cluster", ((cluster_total * rank_size, row_width), bf16), [IN_SMEM, IN_SMEM, IN_VMEM], flops=COST
    )(far_clusters, (fault_pos // GROUP)[None], far_basis)
    far_all = gathered(far_by_cluster)
    deficit, far_by_cluster = lax.optimization_barrier((deficit, far_by_cluster))
    partial_value = call(
        functools.partial(partial_kernel, parts), "partial", ((local_members, rank_size), f32), [IN_SMEM] + [IN_VMEM] * (1 + parts), flops=COST
    )(member_pos[None], deficit, *columns)
    deficit_all = jnp.concatenate(deficits, axis=0)

    total = partial_value + swapped(partial_value, "fault", lambda i: i ^ 1)
    near_side = swapped(deficit_all, "fault", lambda i: i ^ 1)
    far_side = swapped(deficit_all, "fault", lambda i: i + 1 if i % 2 else i - 1)
    bit = 2
    while bit < GROUP:
        total = total + swapped(total, "fault", lambda i: i ^ bit)
        bit *= 2
    low, far_side, near_side = lax.optimization_barrier((total.astype(bf16), far_side, near_side))

    near_field = call(
        functools.partial(near_kernel, own_panels, total_panels),
        "near",
        ((members, row_width), f32),
        [IN_SMEM] * 3 + [IN_VMEM] * 4,
        mib=8,
        flops=COST,
        scratch=[
            pltpu.VMEM((3 * own_panels + 1, members, PANEL), f32),
            pltpu.VMEM((row_count, members, slots * PANEL), bf16),
        ],
    )(near_columns, near_count, fault_pos[None], deficit_all, near_side, far_side, near_blocks)

    high = None
    while bit < fault_count:
        if high is not None:
            low = jnp.concatenate([low, high], axis=1)
        if 2 * bit == fault_count:
            low, near_field = lax.optimization_barrier((low, near_field))
        high = swapped(low, "fault", lambda i: i ^ bit)
        bit *= 2

    near_field = near_field.reshape(parts, local_members, row_width)
    if parts == 2:
        near_rows = [near_field[0], swapped(near_field[1], "member", lambda i: i ^ 1)]
    else:
        exchanged = lax.all_to_all(near_field, "member", 0, 0)
        near_rows = [exchanged[h] for h in range(parts)]

    velocity = jnp.exp(log_rate)
    state_rate = (jnp.exp(-log_state) - velocity) / slip_distance
    resistance = normal_stress[None, :] * direct_effect + damping * velocity
    scale = time_step / resistance
    base = log_rate - scale * (normal_stress[None, :] * evolution_effect * state_rate)
    state_next = log_state + time_step * state_rate
    rate_next = call(
        functools.partial(last_kernel, parts),
        "last",
        ((local_members, elements), f32),
        [IN_SMEM] + [IN_VMEM] * (4 + 2 * parts),
        flops=COST,
    )(member_pos[None], low, high, *far_all, *near_rows, base, scale)
    return rate_next, state_next


def solution(mesh):
    return jax.shard_map(
        per_device,
        mesh=mesh,
        in_specs=(
            P("member", "fault"),
            P("member", "fault"),
            P("member", "fault"),
            P("member", "fault"),
            P("member", "fault"),
            P("fault"),
            P(("fault", "member"), None, None, None),
            P(("fault", "member"), None),
            P(("fault", "member")),
            P(("fault", "member"), None),
            P(("fault", "member"), None, None, None),
            P(None, ("fault", "member")),
        ),
        out_specs=(P("member", "fault"), P("member", "fault")),
        check_vma=False,
    )
```

```python
import functools

import jax
import jax.numpy as jnp
from jax import lax
from jax.experimental import pallas as pl
from jax.experimental.pallas import tpu as pltpu
from jax.sharding import PartitionSpec as P

PANEL = 128
GROUP = 4
COST = 10**9


damping = 0.5
time_step = 0.25

IN_SMEM = pl.BlockSpec(memory_space=pltpu.SMEM)
IN_HBM = pl.BlockSpec(memory_space=pltpu.HBM)
IN_VMEM = pl.BlockSpec(memory_space=pltpu.VMEM)
f32 = jnp.float32
bf16 = jnp.bfloat16


def swapped(block, axis, partner):
    count = lax.axis_size(axis)
    return lax.ppermute(block, axis, [(i, partner(i) % count) for i in range(count)])


def in_hbm(block):
    return pltpu.with_memory_space_constraint(block, pltpu.HBM)


def place_of(parts, pos, h):
    return pos ^ h if parts == 2 else h


def span(start, width):
    return pl.ds(pl.multiple_of(start, PANEL), width)


def pack_kernel(rate_hbm, column_hbm, deficit_ref, message_ref, rate_ref, sems):
    rank, width = column_hbm.shape
    rate_copy = pltpu.make_async_copy(rate_hbm, rate_ref, sems.at[0])
    column_copy = pltpu.make_async_copy(column_hbm, message_ref.at[pl.ds(0, rank)], sems.at[1])
    rate_copy.start()
    column_copy.start()
    rate_copy.wait()
    deficit = (1.0 - jnp.exp(rate_ref[...])).astype(bf16)
    deficit_ref[...] = deficit
    wide = deficit.astype(f32)
    pieces = [wide[:, k : k + width] for k in range(0, wide.shape[1], width)]
    message_ref[rank:] = jnp.concatenate(pieces, axis=0).astype(bf16)
    column_copy.wait()


def partial_kernel(parts, rank, pos_ref, deficit_ref, *refs):
    messages, (all_ref, out_ref) = refs[:parts], refs[parts:]
    local_members = deficit_ref.shape[0]
    total = None
    every = []
    for h in range(parts):
        width = messages[h].shape[1]
        piece = lax.dot_general(
            deficit_ref[:, span(place_of(parts, pos_ref[0], h) * width, width)],
            messages[h][:rank],
            (((1,), (1,)), ((), ())),
            preferred_element_type=f32,
        )
        total = piece if total is None else total + piece
        tail = messages[h][rank:].astype(f32)
        cut = [tail[k : k + local_members] for k in range(0, tail.shape[0], local_members)]
        every.append(jnp.concatenate(cut, axis=1))
    out_ref[...] = total
    all_ref[...] = jnp.concatenate(every, axis=0).astype(bf16)


def far_kernel(cluster_ref, own_cluster_ref, basis_ref, out_ref):
    rows, slots, rank, panel = basis_ref.shape
    clusters = out_ref.shape[0] // rank
    for r in range(rows):
        for j in range(clusters):
            wanted = own_cluster_ref[0] ^ j
            block = jnp.zeros((rank, panel), f32)
            for k in range(slots):
                live = cluster_ref[r, k] == wanted
                block = jnp.where(live, basis_ref[r, k].astype(f32), block)
            out_ref[j * rank : (j + 1) * rank, r * panel : (r + 1) * panel] = block.astype(bf16)


def near_kernel(own_panels, total_panels, column_ref, count_ref, pos_ref, own_ref, near_ref, far_ref, blocks_ref, out_ref, window, picked):
    rows, slots = column_ref.shape
    members = own_ref.shape[0]
    odd = pos_ref[0] % 2
    for side, start in ((own_ref, own_panels), (near_ref, (1 - odd) * 2 * own_panels), (far_ref, odd * 2 * own_panels)):
        for j in range(own_panels):
            window[start + j] = side[:, j * PANEL : (j + 1) * PANEL].astype(f32)
    window[3 * own_panels] = jnp.zeros((members, PANEL), f32)
    base = (pos_ref[0] - 1) * own_panels
    for r in range(rows):
        for s in range(slots):
            place = lax.rem(column_ref[r, s] - base + total_panels, total_panels)
            place = jnp.where(s < count_ref[r], place, 3 * own_panels)
            picked[r, :, s * PANEL : (s + 1) * PANEL] = window[place].astype(bf16)
        out_ref[:, r * PANEL : (r + 1) * PANEL] = jnp.dot(
            picked[r], blocks_ref[r].reshape(slots * PANEL, PANEL), preferred_element_type=f32
        )


def last_kernel(parts, pos_ref, low_ref, high_ref, *refs):
    far_refs, near_refs = refs[:parts], refs[parts : 2 * parts]
    base_ref, scale_ref, out_ref = refs[2 * parts :]
    depth = low_ref.shape[1]
    for h in range(parts):
        width = near_refs[h].shape[1]
        lanes = span(place_of(parts, pos_ref[0], h) * width, width)
        stress = (
            near_refs[h][...]
            + jnp.dot(low_ref[...], far_refs[h][:depth], preferred_element_type=f32)
            + jnp.dot(high_ref[...], far_refs[h][depth:], preferred_element_type=f32)
        )
        out_ref[:, lanes] = base_ref[:, lanes] + scale_ref[:, lanes] * stress


def per_device(
    log_rate,
    log_state,
    direct_effect,
    evolution_effect,
    slip_distance,
    normal_stress,
    near_blocks,
    near_columns,
    near_count,
    far_clusters,
    far_basis,
    column_basis,
):
    fault_count = lax.axis_size("fault")
    parts = lax.axis_size("member")
    fault_pos = lax.axis_index("fault")
    member_pos = lax.axis_index("member")
    local_members, elements = log_rate.shape
    own_panels = elements // PANEL
    total_panels = own_panels * fault_count
    row_count, slots = near_columns.shape
    row_width = row_count * PANEL
    rank_size = column_basis.shape[0]
    cluster_total = fault_count // GROUP
    members = parts * local_members
    def gathered(block):
        if parts == 2:
            return [block, swapped(block, "member", lambda i: i ^ 1)]
        every = lax.all_gather(block, "member", axis=0)
        return [every[h] for h in range(parts)]

    def call(body, name, out_shape, specs, mib=2, flops=10**6, scratch=()):
        return pl.pallas_call(
            body,
            out_shape=[jax.ShapeDtypeStruct(*o) for o in out_shape],
            in_specs=specs,
            out_specs=[IN_VMEM] * len(out_shape),
            scratch_shapes=scratch,
            compiler_params=pltpu.CompilerParams(vmem_limit_bytes=mib << 20),
            cost_estimate=pl.CostEstimate(flops=flops, bytes_accessed=1, transcendentals=0),
            name=name,
        )

    width = column_basis.shape[1]
    deficit, message = call(
        pack_kernel,
        "pack",
        [((local_members, elements), bf16), ((rank_size + members, width), bf16)],
        [IN_HBM] * 2,
        flops=COST,
        scratch=[pltpu.VMEM(log_rate.shape, f32), pltpu.SemaphoreType.DMA((2,))],
    )(in_hbm(log_rate), in_hbm(column_basis))
    messages = gathered(message)
    (far_by_cluster,) = call(
        far_kernel,
        "far_by_cluster",
        [((cluster_total * rank_size, row_width), bf16)],
        [IN_SMEM, IN_SMEM, IN_VMEM],
        flops=COST,
    )(far_clusters, (fault_pos // GROUP)[None], far_basis)
    far_all = gathered(far_by_cluster)
    deficit, far_by_cluster = lax.optimization_barrier((deficit, far_by_cluster))
    deficit_all, partial_value = call(
        functools.partial(partial_kernel, parts, rank_size),
        "partial",
        [((members, elements), bf16), ((local_members, rank_size), f32)],
        [IN_SMEM] + [IN_VMEM] * (1 + parts),
        flops=COST,
    )(member_pos[None], deficit, *messages)

    total = partial_value + swapped(partial_value, "fault", lambda i: i ^ 1)
    near_side = swapped(deficit_all, "fault", lambda i: i ^ 1)
    far_side = swapped(deficit_all, "fault", lambda i: i + 1 if i % 2 else i - 1)
    bit = 2
    while bit < GROUP:
        total = total + swapped(total, "fault", lambda i: i ^ bit ^ 1)
        bit *= 2
    low, near_side = lax.optimization_barrier((total.astype(bf16), near_side))

    (near_field,) = call(
        functools.partial(near_kernel, own_panels, total_panels),
        "near",
        [((members, row_width), f32)],
        [IN_SMEM] * 3 + [IN_VMEM] * 4,
        mib=8,
        flops=COST,
        scratch=[
            pltpu.VMEM((3 * own_panels + 1, members, PANEL), f32),
            pltpu.VMEM((row_count, members, slots * PANEL), bf16),
        ],
    )(near_columns, near_count, fault_pos[None], deficit_all, near_side, far_side, near_blocks)

    high = None
    while bit < fault_count:
        if high is not None:
            low = jnp.concatenate([low, high], axis=1)
        if 2 * bit == fault_count:
            low, near_field = lax.optimization_barrier((low, near_field))
        high = swapped(low, "fault", lambda i: i ^ bit ^ 1)
        bit *= 2

    near_field = near_field.reshape(parts, local_members, row_width)
    if parts == 2:
        near_rows = [near_field[0], swapped(near_field[1], "member", lambda i: i ^ 1)]
    else:
        exchanged = lax.all_to_all(near_field, "member", 0, 0)
        near_rows = [exchanged[h] for h in range(parts)]

    velocity = jnp.exp(log_rate)
    state_rate = (jnp.exp(-log_state) - velocity) / slip_distance
    resistance = normal_stress[None, :] * direct_effect + damping * velocity
    scale = time_step / resistance
    base = log_rate - scale * (normal_stress[None, :] * evolution_effect * state_rate)
    state_next = log_state + time_step * state_rate
    (rate_next,) = call(
        functools.partial(last_kernel, parts),
        "last",
        [((local_members, elements), f32)],
        [IN_SMEM] + [IN_VMEM] * (4 + 2 * parts),
        flops=COST,
    )(member_pos[None], low, high, *far_all, *near_rows, base, scale)
    return rate_next, state_next


def solution(mesh):
    return jax.shard_map(
        per_device,
        mesh=mesh,
        in_specs=(
            P("member", "fault"),
            P("member", "fault"),
            P("member", "fault"),
            P("member", "fault"),
            P("member", "fault"),
            P("fault"),
            P(("fault", "member"), None, None, None),
            P(("fault", "member"), None),
            P(("fault", "member")),
            P(("fault", "member"), None),
            P(("fault", "member"), None, None, None),
            P(None, ("fault", "member")),
        ),
        out_specs=(P("member", "fault"), P("member", "fault")),
        check_vma=False,
    )
```

```python
import functools

import jax
import jax.numpy as jnp
from jax import lax
from jax.experimental import pallas as pl
from jax.experimental.pallas import tpu as pltpu
from jax.sharding import PartitionSpec as P

PANEL = 128
GROUP = 4
COST = 10**9


damping = 0.5
time_step = 0.25

IN_SMEM = pl.BlockSpec(memory_space=pltpu.SMEM)
IN_HBM = pl.BlockSpec(memory_space=pltpu.HBM)
IN_VMEM = pl.BlockSpec(memory_space=pltpu.VMEM)
f32 = jnp.float32
bf16 = jnp.bfloat16


def swapped(block, axis, partner):
    count = lax.axis_size(axis)
    return lax.ppermute(block, axis, [(i, partner(i) % count) for i in range(count)])


def in_hbm(block):
    return pltpu.with_memory_space_constraint(block, pltpu.HBM)


def place_of(parts, pos, h):
    return pos ^ h if parts == 2 else h


def span(start, width):
    return pl.ds(pl.multiple_of(start, PANEL), width)


def deficit_kernel(rate_ref, out_ref):
    out_ref[...] = (1.0 - jnp.exp(rate_ref[...])).astype(bf16)


def partial_kernel(parts, pos_ref, deficit_ref, *refs):
    column_refs, out_ref = refs[:parts], refs[parts]
    total = None
    for h in range(parts):
        width = column_refs[h].shape[1]
        piece = lax.dot_general(
            deficit_ref[:, span(place_of(parts, pos_ref[0], h) * width, width)],
            column_refs[h][...],
            (((1,), (1,)), ((), ())),
            preferred_element_type=f32,
        )
        total = piece if total is None else total + piece
    out_ref[...] = total


def far_kernel(cluster_ref, own_cluster_ref, basis_ref, out_ref):
    rows, slots, rank, panel = basis_ref.shape
    clusters = out_ref.shape[0] // rank
    for r in range(rows):
        for j in range(clusters):
            wanted = own_cluster_ref[0] ^ j
            block = jnp.zeros((rank, panel), f32)
            for k in range(slots):
                live = cluster_ref[r, k] == wanted
                block = jnp.where(live, basis_ref[r, k].astype(f32), block)
            out_ref[j * rank : (j + 1) * rank, r * panel : (r + 1) * panel] = block.astype(bf16)


def near_kernel(own_panels, total_panels, column_ref, count_ref, pos_ref, own_ref, near_ref, far_ref, blocks_ref, out_ref, window, picked):
    rows, slots = column_ref.shape
    members = own_ref.shape[0]
    odd = pos_ref[0] % 2
    for side, start in ((own_ref, own_panels), (near_ref, (1 - odd) * 2 * own_panels), (far_ref, odd * 2 * own_panels)):
        for j in range(own_panels):
            window[start + j] = side[:, j * PANEL : (j + 1) * PANEL].astype(f32)
    window[3 * own_panels] = jnp.zeros((members, PANEL), f32)
    base = (pos_ref[0] - 1) * own_panels
    for r in range(rows):
        for s in range(slots):
            place = lax.rem(column_ref[r, s] - base + total_panels, total_panels)
            place = jnp.where(s < count_ref[r], place, 3 * own_panels)
            picked[r, :, s * PANEL : (s + 1) * PANEL] = window[place].astype(bf16)
        out_ref[:, r * PANEL : (r + 1) * PANEL] = jnp.dot(
            picked[r], blocks_ref[r].reshape(slots * PANEL, PANEL), preferred_element_type=f32
        )


def last_kernel(parts, pos_ref, low_ref, high_ref, *refs):
    far_refs, near_refs = refs[:parts], refs[parts : 2 * parts]
    base_ref, scale_ref, out_ref = refs[2 * parts :]
    depth = low_ref.shape[1]
    for h in range(parts):
        width = near_refs[h].shape[1]
        lanes = span(place_of(parts, pos_ref[0], h) * width, width)
        stress = (
            near_refs[h][...]
            + jnp.dot(low_ref[...], far_refs[h][:depth], preferred_element_type=f32)
            + jnp.dot(high_ref[...], far_refs[h][depth:], preferred_element_type=f32)
        )
        out_ref[:, lanes] = base_ref[:, lanes] + scale_ref[:, lanes] * stress


def per_device(
    log_rate,
    log_state,
    direct_effect,
    evolution_effect,
    slip_distance,
    normal_stress,
    near_blocks,
    near_columns,
    near_count,
    far_clusters,
    far_basis,
    column_basis,
):
    fault_count = lax.axis_size("fault")
    parts = lax.axis_size("member")
    fault_pos = lax.axis_index("fault")
    member_pos = lax.axis_index("member")
    local_members, elements = log_rate.shape
    own_panels = elements // PANEL
    total_panels = own_panels * fault_count
    row_count, slots = near_columns.shape
    row_width = row_count * PANEL
    rank_size = column_basis.shape[0]
    cluster_total = fault_count // GROUP
    members = parts * local_members
    def gathered(block):
        if parts == 2:
            return [block, swapped(block, "member", lambda i: i ^ 1)]
        every = lax.all_gather(block, "member", axis=0)
        return [every[h] for h in range(parts)]

    def call(body, name, out_shape, specs, mib=2, flops=10**6, scratch=()):
        return pl.pallas_call(
            body,
            out_shape=[jax.ShapeDtypeStruct(*o) for o in out_shape],
            in_specs=specs,
            out_specs=[IN_VMEM] * len(out_shape),
            scratch_shapes=scratch,
            compiler_params=pltpu.CompilerParams(vmem_limit_bytes=mib << 20),
            cost_estimate=pl.CostEstimate(flops=flops, bytes_accessed=1, transcendentals=0),
            name=name,
        )

    if parts == 2:
        other = swapped(in_hbm(column_basis), "member", lambda i: i ^ 1)
        columns = [column_basis, pltpu.with_memory_space_constraint(other, pltpu.VMEM)]
    else:
        columns = gathered(column_basis)
    (far_by_cluster,) = call(
        far_kernel,
        "far_by_cluster",
        [((cluster_total * rank_size, row_width), bf16)],
        [IN_SMEM, IN_SMEM, IN_VMEM],
        flops=COST,
    )(in_hbm(far_clusters), (fault_pos // GROUP)[None], in_hbm(far_basis))
    far_all = gathered(far_by_cluster)
    log_rate_later, far_by_cluster = lax.optimization_barrier((log_rate, far_by_cluster))
    (deficit,) = call(
        deficit_kernel, "deficit", [((local_members, elements), bf16)], [IN_VMEM], flops=COST
    )(log_rate_later)
    deficit_all = jnp.concatenate(gathered(deficit), axis=0)
    (partial_value,) = call(
        functools.partial(partial_kernel, parts),
        "partial",
        [((local_members, rank_size), f32)],
        [IN_SMEM] + [IN_VMEM] * (1 + parts),
        flops=COST,
    )(member_pos[None], deficit, *columns)

    total = partial_value + swapped(partial_value, "fault", lambda i: i ^ 1)
    near_side = swapped(deficit_all, "fault", lambda i: i ^ 1)
    far_side = swapped(deficit_all, "fault", lambda i: i + 1 if i % 2 else i - 1)
    bit = 2
    while bit < GROUP:
        total = total + swapped(total, "fault", lambda i: i ^ bit ^ 1)
        bit *= 2
    low, near_side = lax.optimization_barrier((total.astype(bf16), near_side))

    (near_field,) = call(
        functools.partial(near_kernel, own_panels, total_panels),
        "near",
        [((members, row_width), f32)],
        [IN_SMEM] * 3 + [IN_VMEM] * 4,
        mib=8,
        flops=COST,
        scratch=[
            pltpu.VMEM((3 * own_panels + 1, members, PANEL), f32),
            pltpu.VMEM((row_count, members, slots * PANEL), bf16),
        ],
    )(near_columns, near_count, fault_pos[None], deficit_all, near_side, far_side, near_blocks)

    high = None
    while bit < fault_count:
        if high is not None:
            low = jnp.concatenate([low, high], axis=1)
        if 2 * bit == fault_count:
            low, near_field = lax.optimization_barrier((low, near_field))
        high = swapped(low, "fault", lambda i: i ^ bit ^ 1)
        bit *= 2

    near_field = near_field.reshape(parts, local_members, row_width)
    if parts == 2:
        near_rows = [near_field[0], swapped(near_field[1], "member", lambda i: i ^ 1)]
    else:
        exchanged = lax.all_to_all(near_field, "member", 0, 0)
        near_rows = [exchanged[h] for h in range(parts)]

    velocity = jnp.exp(log_rate)
    state_rate = (jnp.exp(-log_state) - velocity) / slip_distance
    resistance = normal_stress[None, :] * direct_effect + damping * velocity
    scale = time_step / resistance
    base = log_rate - scale * (normal_stress[None, :] * evolution_effect * state_rate)
    state_next = log_state + time_step * state_rate
    (rate_next,) = call(
        functools.partial(last_kernel, parts),
        "last",
        [((local_members, elements), f32)],
        [IN_SMEM] + [IN_VMEM] * (4 + 2 * parts),
        flops=COST,
    )(member_pos[None], low, high, *far_all, *near_rows, base, scale)
    return rate_next, state_next


def solution(mesh):
    return jax.shard_map(
        per_device,
        mesh=mesh,
        in_specs=(
            P("member", "fault"),
            P("member", "fault"),
            P("member", "fault"),
            P("member", "fault"),
            P("member", "fault"),
            P("fault"),
            P(("fault", "member"), None, None, None),
            P(("fault", "member"), None),
            P(("fault", "member")),
            P(("fault", "member"), None),
            P(("fault", "member"), None, None, None),
            P(None, ("fault", "member")),
        ),
        out_specs=(P("member", "fault"), P("member", "fault")),
        check_vma=False,
    )
```

```python
import functools

import jax
import jax.numpy as jnp
from jax import lax
from jax.experimental import pallas as pl
from jax.experimental.pallas import tpu as pltpu
from jax.sharding import PartitionSpec as P

PANEL = 128
GROUP = 4
COST = 10**9


damping = 0.5
time_step = 0.25

IN_SMEM = pl.BlockSpec(memory_space=pltpu.SMEM)
IN_HBM = pl.BlockSpec(memory_space=pltpu.HBM)
IN_VMEM = pl.BlockSpec(memory_space=pltpu.VMEM)
f32 = jnp.float32
bf16 = jnp.bfloat16


def swapped(block, axis, partner):
    count = lax.axis_size(axis)
    return lax.ppermute(block, axis, [(i, partner(i) % count) for i in range(count)])


def in_hbm(block):
    return pltpu.with_memory_space_constraint(block, pltpu.HBM)


def place_of(parts, pos, h):
    return pos ^ h if parts == 2 else h


def span(start, width):
    return pl.ds(pl.multiple_of(start, PANEL), width)


def deficit_kernel(rate_ref, out_ref):
    out_ref[...] = (1.0 - jnp.exp(rate_ref[...])).astype(bf16)


def partial_kernel(parts, pos_ref, deficit_ref, *refs):
    column_refs, out_ref = refs[:parts], refs[parts]
    total = None
    for h in range(parts):
        width = column_refs[h].shape[1]
        piece = lax.dot_general(
            deficit_ref[:, span(place_of(parts, pos_ref[0], h) * width, width)],
            column_refs[h][...],
            (((1,), (1,)), ((), ())),
            preferred_element_type=f32,
        )
        total = piece if total is None else total + piece
    out_ref[...] = total


def far_kernel(cluster_ref, own_cluster_ref, basis_ref, out_ref):
    rows, slots, rank, panel = basis_ref.shape
    clusters = out_ref.shape[0] // rank
    for r in range(rows):
        for j in range(clusters):
            wanted = own_cluster_ref[0] ^ j
            block = jnp.zeros((rank, panel), f32)
            for k in range(slots):
                live = cluster_ref[r, k] == wanted
                block = jnp.where(live, basis_ref[r, k].astype(f32), block)
            out_ref[j * rank : (j + 1) * rank, r * panel : (r + 1) * panel] = block.astype(bf16)


def near_kernel(own_panels, total_panels, column_ref, count_ref, pos_ref, own_ref, near_ref, far_ref, blocks_ref, out_ref, window):
    rows, slots = column_ref.shape
    members = own_ref.shape[0]
    odd = pos_ref[0] % 2
    for side, start in ((own_ref, own_panels), (near_ref, (1 - odd) * 2 * own_panels), (far_ref, odd * 2 * own_panels)):
        for j in range(own_panels):
            window[start + j] = side[:, j * PANEL : (j + 1) * PANEL].astype(f32)
    window[3 * own_panels] = jnp.zeros((members, PANEL), f32)
    base = (pos_ref[0] - 1) * own_panels
    for r in range(rows):
        tiles = []
        for s in range(slots):
            place = lax.rem(column_ref[r, s] - base + total_panels, total_panels)
            tiles.append(window[jnp.where(s < count_ref[r], place, 3 * own_panels)])
        out_ref[:, r * PANEL : (r + 1) * PANEL] = jnp.dot(
            jnp.concatenate(tiles, axis=1).astype(bf16),
            blocks_ref[r].reshape(slots * PANEL, PANEL),
            preferred_element_type=f32,
        )


def last_kernel(parts, pos_ref, low_ref, high_ref, *refs):
    far_refs, near_refs = refs[:parts], refs[parts : 2 * parts]
    base_ref, scale_ref, out_ref = refs[2 * parts :]
    depth = low_ref.shape[1]
    for h in range(parts):
        width = near_refs[h].shape[1]
        lanes = span(place_of(parts, pos_ref[0], h) * width, width)
        stress = (
            near_refs[h][...]
            + jnp.dot(low_ref[...], far_refs[h][:depth], preferred_element_type=f32)
            + jnp.dot(high_ref[...], far_refs[h][depth:], preferred_element_type=f32)
        )
        out_ref[:, lanes] = base_ref[:, lanes] + scale_ref[:, lanes] * stress


def per_device(
    log_rate,
    log_state,
    direct_effect,
    evolution_effect,
    slip_distance,
    normal_stress,
    near_blocks,
    near_columns,
    near_count,
    far_clusters,
    far_basis,
    column_basis,
):
    fault_count = lax.axis_size("fault")
    parts = lax.axis_size("member")
    fault_pos = lax.axis_index("fault")
    member_pos = lax.axis_index("member")
    local_members, elements = log_rate.shape
    own_panels = elements // PANEL
    total_panels = own_panels * fault_count
    row_count, slots = near_columns.shape
    row_width = row_count * PANEL
    rank_size = column_basis.shape[0]
    cluster_total = fault_count // GROUP
    members = parts * local_members
    def gathered(block):
        if parts == 2:
            return [block, swapped(block, "member", lambda i: i ^ 1)]
        every = lax.all_gather(block, "member", axis=0)
        return [every[h] for h in range(parts)]

    def call(body, name, out_shape, specs, mib=2, flops=10**6, scratch=()):
        return pl.pallas_call(
            body,
            out_shape=[jax.ShapeDtypeStruct(*o) for o in out_shape],
            in_specs=specs,
            out_specs=[IN_VMEM] * len(out_shape),
            scratch_shapes=scratch,
            compiler_params=pltpu.CompilerParams(vmem_limit_bytes=mib << 20),
            cost_estimate=pl.CostEstimate(flops=flops, bytes_accessed=1, transcendentals=0),
            name=name,
        )

    if parts == 2:
        other = swapped(in_hbm(column_basis), "member", lambda i: i ^ 1)
        columns = [column_basis, pltpu.with_memory_space_constraint(other, pltpu.VMEM)]
    else:
        columns = gathered(column_basis)
    (far_by_cluster,) = call(
        far_kernel,
        "far_by_cluster",
        [((cluster_total * rank_size, row_width), bf16)],
        [IN_SMEM, IN_SMEM, IN_VMEM],
        flops=COST,
    )(in_hbm(far_clusters), (fault_pos // GROUP)[None], in_hbm(far_basis))
    log_rate_later, far_by_cluster = lax.optimization_barrier((log_rate, far_by_cluster))
    (deficit,) = call(
        deficit_kernel, "deficit", [((local_members, elements), bf16)], [IN_VMEM], flops=COST
    )(log_rate_later)
    deficit_all = jnp.concatenate(gathered(deficit), axis=0)
    (partial_value,) = call(
        functools.partial(partial_kernel, parts),
        "partial",
        [((local_members, rank_size), f32)],
        [IN_SMEM] + [IN_VMEM] * (1 + parts),
        flops=COST,
    )(member_pos[None], deficit, *columns)

    total = partial_value + swapped(partial_value, "fault", lambda i: i ^ 1)
    near_side = swapped(deficit_all, "fault", lambda i: i ^ 1)
    far_side = swapped(deficit_all, "fault", lambda i: i + 1 if i % 2 else i - 1)
    bit = 2
    while bit < GROUP:
        total = total + swapped(total, "fault", lambda i: i ^ bit ^ 1)
        bit *= 2
    low, near_side, far_by_cluster = lax.optimization_barrier((total.astype(bf16), near_side, far_by_cluster))
    far_all = gathered(far_by_cluster)

    (near_field,) = call(
        functools.partial(near_kernel, own_panels, total_panels),
        "near",
        [((members, row_width), f32)],
        [IN_SMEM] * 3 + [IN_VMEM] * 4,
        mib=8,
        flops=COST,
        scratch=[pltpu.VMEM((3 * own_panels + 1, members, PANEL), f32)],
    )(near_columns, near_count, fault_pos[None], deficit_all, near_side, far_side, near_blocks)

    high = None
    while bit < fault_count:
        if high is not None:
            low = jnp.concatenate([low, high], axis=1)
        if 2 * bit == fault_count:
            low, near_field = lax.optimization_barrier((low, near_field))
        high = swapped(low, "fault", lambda i: i ^ bit ^ 1)
        bit *= 2

    near_field = near_field.reshape(parts, local_members, row_width)
    if parts == 2:
        near_rows = [near_field[0], swapped(near_field[1], "member", lambda i: i ^ 1)]
    else:
        exchanged = lax.all_to_all(near_field, "member", 0, 0)
        near_rows = [exchanged[h] for h in range(parts)]

    velocity = jnp.exp(log_rate)
    state_rate = (jnp.exp(-log_state) - velocity) / slip_distance
    resistance = normal_stress[None, :] * direct_effect + damping * velocity
    scale = time_step / resistance
    base = log_rate - scale * (normal_stress[None, :] * evolution_effect * state_rate)
    state_next = log_state + time_step * state_rate
    (rate_next,) = call(
        functools.partial(last_kernel, parts),
        "last",
        [((local_members, elements), f32)],
        [IN_SMEM] + [IN_VMEM] * (4 + 2 * parts),
        flops=COST,
    )(member_pos[None], low, high, *far_all, *near_rows, base, scale)
    return rate_next, state_next


def solution(mesh):
    return jax.shard_map(
        per_device,
        mesh=mesh,
        in_specs=(
            P("member", "fault"),
            P("member", "fault"),
            P("member", "fault"),
            P("member", "fault"),
            P("member", "fault"),
            P("fault"),
            P(("fault", "member"), None, None, None),
            P(("fault", "member"), None),
            P(("fault", "member")),
            P(("fault", "member"), None),
            P(("fault", "member"), None, None, None),
            P(None, ("fault", "member")),
        ),
        out_specs=(P("member", "fault"), P("member", "fault")),
        check_vma=False,
    )
```

```python
import functools

import jax
import jax.numpy as jnp
from jax import lax
from jax.experimental import pallas as pl
from jax.experimental.pallas import tpu as pltpu
from jax.sharding import PartitionSpec as P

PANEL = 128
GROUP = 4
COST = 10**9


damping = 0.5
time_step = 0.25

IN_SMEM = pl.BlockSpec(memory_space=pltpu.SMEM)
IN_HBM = pl.BlockSpec(memory_space=pltpu.HBM)
IN_VMEM = pl.BlockSpec(memory_space=pltpu.VMEM)
f32 = jnp.float32
bf16 = jnp.bfloat16


def swapped(block, axis, partner):
    count = lax.axis_size(axis)
    return lax.ppermute(block, axis, [(i, partner(i) % count) for i in range(count)])


def in_hbm(block):
    return pltpu.with_memory_space_constraint(block, pltpu.HBM)


def place_of(parts, pos, h):
    return pos ^ h if parts == 2 else h


def span(start, width):
    return pl.ds(pl.multiple_of(start, PANEL), width)


def deficit_kernel(rate_ref, out_ref):
    out_ref[...] = (1.0 - jnp.exp(rate_ref[...])).astype(bf16)


def partial_kernel(parts, pos_ref, deficit_ref, *refs):
    column_refs, out_ref = refs[:parts], refs[parts]
    total = None
    for h in range(parts):
        width = column_refs[h].shape[1]
        piece = lax.dot_general(
            deficit_ref[:, span(place_of(parts, pos_ref[0], h) * width, width)],
            column_refs[h][...],
            (((1,), (1,)), ((), ())),
            preferred_element_type=f32,
        )
        total = piece if total is None else total + piece
    out_ref[...] = total


def far_kernel(cluster_ref, own_cluster_ref, basis_ref, out_ref):
    rows, slots, rank, panel = basis_ref.shape
    clusters = out_ref.shape[0] // rank
    for r in range(rows):
        for j in range(clusters):
            wanted = own_cluster_ref[0] ^ j
            block = jnp.zeros((rank, panel), f32)
            for k in range(slots):
                live = cluster_ref[r, k] == wanted
                block = jnp.where(live, basis_ref[r, k].astype(f32), block)
            out_ref[j * rank : (j + 1) * rank, r * panel : (r + 1) * panel] = block.astype(bf16)


def near_kernel(own_panels, total_panels, column_ref, count_ref, pos_ref, own_ref, near_ref, far_ref, blocks_ref, out_ref, window):
    rows, slots = column_ref.shape
    members = own_ref.shape[0]
    odd = pos_ref[0] % 2
    for side, start in ((own_ref, own_panels), (near_ref, (1 - odd) * 2 * own_panels), (far_ref, odd * 2 * own_panels)):
        for j in range(own_panels):
            window[start + j] = side[:, j * PANEL : (j + 1) * PANEL].astype(f32)
    window[3 * own_panels] = jnp.zeros((members, PANEL), f32)
    base = (pos_ref[0] - 1) * own_panels
    for r in range(rows):
        tiles = []
        for s in range(slots):
            place = lax.rem(column_ref[r, s] - base + total_panels, total_panels)
            tiles.append(window[jnp.where(s < count_ref[r], place, 3 * own_panels)])
        out_ref[:, r * PANEL : (r + 1) * PANEL] = jnp.dot(
            jnp.concatenate(tiles, axis=1).astype(bf16),
            blocks_ref[r].reshape(slots * PANEL, PANEL),
            preferred_element_type=f32,
        )


def last_kernel(parts, pos_ref, low_ref, high_ref, *refs):
    far_refs, near_refs = refs[:parts], refs[parts : 2 * parts]
    base_ref, scale_ref, out_ref = refs[2 * parts :]
    depth = low_ref.shape[1]
    for h in range(parts):
        width = near_refs[h].shape[1]
        lanes = span(place_of(parts, pos_ref[0], h) * width, width)
        stress = (
            near_refs[h][...]
            + jnp.dot(low_ref[...], far_refs[h][:depth], preferred_element_type=f32)
            + jnp.dot(high_ref[...], far_refs[h][depth:], preferred_element_type=f32)
        )
        out_ref[:, lanes] = base_ref[:, lanes] + scale_ref[:, lanes] * stress


def per_device(
    log_rate,
    log_state,
    direct_effect,
    evolution_effect,
    slip_distance,
    normal_stress,
    near_blocks,
    near_columns,
    near_count,
    far_clusters,
    far_basis,
    column_basis,
):
    fault_count = lax.axis_size("fault")
    parts = lax.axis_size("member")
    fault_pos = lax.axis_index("fault")
    member_pos = lax.axis_index("member")
    local_members, elements = log_rate.shape
    own_panels = elements // PANEL
    total_panels = own_panels * fault_count
    row_count, slots = near_columns.shape
    row_width = row_count * PANEL
    rank_size = column_basis.shape[0]
    cluster_total = fault_count // GROUP
    members = parts * local_members
    def gathered(block):
        if parts == 2:
            return [block, swapped(block, "member", lambda i: i ^ 1)]
        every = lax.all_gather(block, "member", axis=0)
        return [every[h] for h in range(parts)]

    def call(body, name, out_shape, specs, mib=2, flops=10**6, scratch=()):
        return pl.pallas_call(
            body,
            out_shape=[jax.ShapeDtypeStruct(*o) for o in out_shape],
            in_specs=specs,
            out_specs=[IN_VMEM] * len(out_shape),
            scratch_shapes=scratch,
            compiler_params=pltpu.CompilerParams(vmem_limit_bytes=mib << 20),
            cost_estimate=pl.CostEstimate(flops=flops, bytes_accessed=1, transcendentals=0),
            name=name,
        )

    if parts == 2:
        other = swapped(in_hbm(column_basis), "member", lambda i: i ^ 1)
        columns = [column_basis, pltpu.with_memory_space_constraint(other, pltpu.VMEM)]
    else:
        columns = gathered(column_basis)
    (far_by_cluster,) = call(
        far_kernel,
        "far_by_cluster",
        [((cluster_total * rank_size, row_width), bf16)],
        [IN_SMEM, IN_SMEM, IN_VMEM],
        flops=COST,
    )(in_hbm(far_clusters), (fault_pos // GROUP)[None], in_hbm(far_basis))
    far_all = gathered(far_by_cluster)
    log_rate_later, far_by_cluster = lax.optimization_barrier((log_rate, far_by_cluster))
    (deficit,) = call(
        deficit_kernel, "deficit", [((local_members, elements), bf16)], [IN_VMEM], flops=COST
    )(log_rate_later)
    deficit_all = jnp.concatenate(gathered(deficit), axis=0)
    (partial_value,) = call(
        functools.partial(partial_kernel, parts),
        "partial",
        [((local_members, rank_size), f32)],
        [IN_SMEM] + [IN_VMEM] * (1 + parts),
        flops=COST,
    )(member_pos[None], deficit, *columns)

    total = partial_value + swapped(partial_value, "fault", lambda i: i ^ 1)
    near_side = swapped(deficit_all, "fault", lambda i: i ^ 1)
    far_side = swapped(deficit_all, "fault", lambda i: i + 1 if i % 2 else i - 1)
    bit = 2
    while bit < GROUP:
        total = total + swapped(total, "fault", lambda i: i ^ bit ^ 1)
        bit *= 2
    low = total.astype(bf16)

    (near_field,) = call(
        functools.partial(near_kernel, own_panels, total_panels),
        "near",
        [((members, row_width), f32)],
        [IN_SMEM] * 3 + [IN_VMEM] * 4,
        mib=8,
        flops=COST,
        scratch=[pltpu.VMEM((3 * own_panels + 1, members, PANEL), f32)],
    )(near_columns, near_count, fault_pos[None], deficit_all, near_side, far_side, near_blocks)

    high = None
    while bit < fault_count:
        if high is not None:
            low = jnp.concatenate([low, high], axis=1)
        if 2 * bit == fault_count:
            low, near_field = lax.optimization_barrier((low, near_field))
        high = swapped(low, "fault", lambda i: i ^ bit ^ 1)
        bit *= 2

    near_field = near_field.reshape(parts, local_members, row_width)
    if parts == 2:
        near_rows = [near_field[0], swapped(near_field[1], "member", lambda i: i ^ 1)]
    else:
        exchanged = lax.all_to_all(near_field, "member", 0, 0)
        near_rows = [exchanged[h] for h in range(parts)]

    velocity = jnp.exp(log_rate)
    state_rate = (jnp.exp(-log_state) - velocity) / slip_distance
    resistance = normal_stress[None, :] * direct_effect + damping * velocity
    scale = time_step / resistance
    base = log_rate - scale * (normal_stress[None, :] * evolution_effect * state_rate)
    state_next = log_state + time_step * state_rate
    (rate_next,) = call(
        functools.partial(last_kernel, parts),
        "last",
        [((local_members, elements), f32)],
        [IN_SMEM] + [IN_VMEM] * (4 + 2 * parts),
        flops=COST,
    )(member_pos[None], low, high, *far_all, *near_rows, base, scale)
    return rate_next, state_next


def solution(mesh):
    return jax.shard_map(
        per_device,
        mesh=mesh,
        in_specs=(
            P("member", "fault"),
            P("member", "fault"),
            P("member", "fault"),
            P("member", "fault"),
            P("member", "fault"),
            P("fault"),
            P(("fault", "member"), None, None, None),
            P(("fault", "member"), None),
            P(("fault", "member")),
            P(("fault", "member"), None),
            P(("fault", "member"), None, None, None),
            P(None, ("fault", "member")),
        ),
        out_specs=(P("member", "fault"), P("member", "fault")),
        check_vma=False,
    )
```

```python
import functools

import jax
import jax.numpy as jnp
from jax import lax
from jax.experimental import pallas as pl
from jax.experimental.pallas import tpu as pltpu
from jax.sharding import PartitionSpec as P

PANEL = 128
GROUP = 4
COST = 10**9


damping = 0.5
time_step = 0.25

IN_SMEM = pl.BlockSpec(memory_space=pltpu.SMEM)
IN_HBM = pl.BlockSpec(memory_space=pltpu.HBM)
IN_VMEM = pl.BlockSpec(memory_space=pltpu.VMEM)
f32 = jnp.float32
bf16 = jnp.bfloat16


def swapped(block, axis, partner):
    count = lax.axis_size(axis)
    return lax.ppermute(block, axis, [(i, partner(i) % count) for i in range(count)])


def in_hbm(block):
    return pltpu.with_memory_space_constraint(block, pltpu.HBM)


def place_of(parts, pos, h):
    return pos ^ h if parts == 2 else h


def span(start, width):
    return pl.ds(pl.multiple_of(start, PANEL), width)


def deficit_kernel(rate_ref, out_ref):
    out_ref[...] = (1.0 - jnp.exp(rate_ref[...])).astype(bf16)


def partial_kernel(parts, pos_ref, deficit_ref, *refs):
    column_refs, out_ref = refs[:parts], refs[parts]
    total = None
    for h in range(parts):
        width = column_refs[h].shape[1]
        piece = lax.dot_general(
            deficit_ref[:, span(place_of(parts, pos_ref[0], h) * width, width)],
            column_refs[h][...],
            (((1,), (1,)), ((), ())),
            preferred_element_type=f32,
        )
        total = piece if total is None else total + piece
    out_ref[...] = total


def far_kernel(cluster_ref, own_cluster_ref, basis_ref, out_ref):
    rows, slots, rank, panel = basis_ref.shape
    clusters = out_ref.shape[0] // rank
    for r in range(rows):
        for j in range(clusters):
            wanted = own_cluster_ref[0] ^ j
            block = jnp.zeros((rank, panel), f32)
            for k in range(slots):
                live = cluster_ref[r, k] == wanted
                block = jnp.where(live, basis_ref[r, k].astype(f32), block)
            out_ref[j * rank : (j + 1) * rank, r * panel : (r + 1) * panel] = block.astype(bf16)


def near_kernel(own_panels, total_panels, column_ref, count_ref, pos_ref, own_ref, near_ref, far_ref, blocks_ref, out_ref, window):
    rows, slots = column_ref.shape
    members = own_ref.shape[0]
    odd = pos_ref[0] % 2
    for side, start in ((own_ref, own_panels), (near_ref, (1 - odd) * 2 * own_panels), (far_ref, odd * 2 * own_panels)):
        for j in range(own_panels):
            window[start + j] = side[:, j * PANEL : (j + 1) * PANEL].astype(f32)
    window[3 * own_panels] = jnp.zeros((members, PANEL), f32)
    base = (pos_ref[0] - 1) * own_panels
    for r in range(rows):
        total = None
        for s0 in range(0, slots, 2):
            tiles = []
            for s in range(s0, min(s0 + 2, slots)):
                place = lax.rem(column_ref[r, s] - base + total_panels, total_panels)
                tiles.append(window[jnp.where(s < count_ref[r], place, 3 * own_panels)])
            piece = jnp.dot(
                jnp.concatenate(tiles, axis=1).astype(bf16),
                blocks_ref[r, s0 : s0 + 2].reshape(len(tiles) * PANEL, PANEL),
                preferred_element_type=f32,
            )
            total = piece if total is None else total + piece
        out_ref[:, r * PANEL : (r + 1) * PANEL] = total


def last_kernel(parts, pos_ref, low_ref, high_ref, *refs):
    far_refs, near_refs = refs[:parts], refs[parts : 2 * parts]
    base_ref, scale_ref, out_ref = refs[2 * parts :]
    depth = low_ref.shape[1]
    for h in range(parts):
        width = near_refs[h].shape[1]
        lanes = span(place_of(parts, pos_ref[0], h) * width, width)
        stress = (
            near_refs[h][...]
            + jnp.dot(low_ref[...], far_refs[h][:depth], preferred_element_type=f32)
            + jnp.dot(high_ref[...], far_refs[h][depth:], preferred_element_type=f32)
        )
        out_ref[:, lanes] = base_ref[:, lanes] + scale_ref[:, lanes] * stress


def per_device(
    log_rate,
    log_state,
    direct_effect,
    evolution_effect,
    slip_distance,
    normal_stress,
    near_blocks,
    near_columns,
    near_count,
    far_clusters,
    far_basis,
    column_basis,
):
    fault_count = lax.axis_size("fault")
    parts = lax.axis_size("member")
    fault_pos = lax.axis_index("fault")
    member_pos = lax.axis_index("member")
    local_members, elements = log_rate.shape
    own_panels = elements // PANEL
    total_panels = own_panels * fault_count
    row_count, slots = near_columns.shape
    row_width = row_count * PANEL
    rank_size = column_basis.shape[0]
    cluster_total = fault_count // GROUP
    members = parts * local_members
    def gathered(block):
        if parts == 2:
            return [block, swapped(block, "member", lambda i: i ^ 1)]
        every = lax.all_gather(block, "member", axis=0)
        return [every[h] for h in range(parts)]

    def call(body, name, out_shape, specs, mib=2, flops=10**6, scratch=()):
        return pl.pallas_call(
            body,
            out_shape=[jax.ShapeDtypeStruct(*o) for o in out_shape],
            in_specs=specs,
            out_specs=[IN_VMEM] * len(out_shape),
            scratch_shapes=scratch,
            compiler_params=pltpu.CompilerParams(vmem_limit_bytes=mib << 20),
            cost_estimate=pl.CostEstimate(flops=flops, bytes_accessed=1, transcendentals=0),
            name=name,
        )

    if parts == 2:
        other = swapped(in_hbm(column_basis), "member", lambda i: i ^ 1)
        columns = [column_basis, pltpu.with_memory_space_constraint(other, pltpu.VMEM)]
    else:
        columns = gathered(column_basis)
    (far_by_cluster,) = call(
        far_kernel,
        "far_by_cluster",
        [((cluster_total * rank_size, row_width), bf16)],
        [IN_SMEM, IN_SMEM, IN_VMEM],
        flops=COST,
    )(in_hbm(far_clusters), (fault_pos // GROUP)[None], in_hbm(far_basis))
    far_all = gathered(far_by_cluster)
    log_rate_later, far_by_cluster = lax.optimization_barrier((log_rate, far_by_cluster))
    (deficit,) = call(
        deficit_kernel, "deficit", [((local_members, elements), bf16)], [IN_VMEM], flops=COST
    )(log_rate_later)
    deficit_all = jnp.concatenate(gathered(deficit), axis=0)
    (partial_value,) = call(
        functools.partial(partial_kernel, parts),
        "partial",
        [((local_members, rank_size), f32)],
        [IN_SMEM] + [IN_VMEM] * (1 + parts),
        flops=COST,
    )(member_pos[None], deficit, *columns)

    total = partial_value + swapped(partial_value, "fault", lambda i: i ^ 1)
    near_side = swapped(deficit_all, "fault", lambda i: i ^ 1)
    far_side = swapped(deficit_all, "fault", lambda i: i + 1 if i % 2 else i - 1)
    bit = 2
    while bit < GROUP:
        total = total + swapped(total, "fault", lambda i: i ^ bit ^ 1)
        bit *= 2
    low = total.astype(bf16)

    (near_field,) = call(
        functools.partial(near_kernel, own_panels, total_panels),
        "near",
        [((members, row_width), f32)],
        [IN_SMEM] * 3 + [IN_VMEM] * 4,
        mib=8,
        flops=COST,
        scratch=[pltpu.VMEM((3 * own_panels + 1, members, PANEL), f32)],
    )(near_columns, near_count, fault_pos[None], deficit_all, near_side, far_side, near_blocks)

    high = None
    while bit < fault_count:
        if high is not None:
            low = jnp.concatenate([low, high], axis=1)
        if 2 * bit == fault_count:
            low, near_field = lax.optimization_barrier((low, near_field))
        high = swapped(low, "fault", lambda i: i ^ bit ^ 1)
        bit *= 2

    near_field = near_field.reshape(parts, local_members, row_width)
    if parts == 2:
        near_rows = [near_field[0], swapped(near_field[1], "member", lambda i: i ^ 1)]
    else:
        exchanged = lax.all_to_all(near_field, "member", 0, 0)
        near_rows = [exchanged[h] for h in range(parts)]

    velocity = jnp.exp(log_rate)
    state_rate = (jnp.exp(-log_state) - velocity) / slip_distance
    resistance = normal_stress[None, :] * direct_effect + damping * velocity
    scale = time_step / resistance
    base = log_rate - scale * (normal_stress[None, :] * evolution_effect * state_rate)
    state_next = log_state + time_step * state_rate
    (rate_next,) = call(
        functools.partial(last_kernel, parts),
        "last",
        [((local_members, elements), f32)],
        [IN_SMEM] + [IN_VMEM] * (4 + 2 * parts),
        flops=COST,
    )(member_pos[None], low, high, *far_all, *near_rows, base, scale)
    return rate_next, state_next


def solution(mesh):
    return jax.shard_map(
        per_device,
        mesh=mesh,
        in_specs=(
            P("member", "fault"),
            P("member", "fault"),
            P("member", "fault"),
            P("member", "fault"),
            P("member", "fault"),
            P("fault"),
            P(("fault", "member"), None, None, None),
            P(("fault", "member"), None),
            P(("fault", "member")),
            P(("fault", "member"), None),
            P(("fault", "member"), None, None, None),
            P(None, ("fault", "member")),
        ),
        out_specs=(P("member", "fault"), P("member", "fault")),
        check_vma=False,
    )
```

```python
import functools

import jax
import jax.numpy as jnp
from jax import lax
from jax.experimental import pallas as pl
from jax.experimental.pallas import tpu as pltpu
from jax.sharding import PartitionSpec as P

PANEL = 128
GROUP = 4
COST = 10**9


damping = 0.5
time_step = 0.25

IN_SMEM = pl.BlockSpec(memory_space=pltpu.SMEM)
IN_HBM = pl.BlockSpec(memory_space=pltpu.HBM)
IN_VMEM = pl.BlockSpec(memory_space=pltpu.VMEM)
f32 = jnp.float32
bf16 = jnp.bfloat16


def swapped(block, axis, partner):
    count = lax.axis_size(axis)
    return lax.ppermute(block, axis, [(i, partner(i) % count) for i in range(count)])


def in_hbm(block):
    return pltpu.with_memory_space_constraint(block, pltpu.HBM)


def place_of(parts, pos, h):
    return pos ^ h if parts == 2 else h


def span(start, width):
    return pl.ds(pl.multiple_of(start, PANEL), width)


def deficit_kernel(rate_ref, out_ref):
    out_ref[...] = (1.0 - jnp.exp(rate_ref[...])).astype(bf16)


def partial_kernel(parts, pos_ref, deficit_ref, *refs):
    column_refs, out_ref = refs[:parts], refs[parts]
    total = None
    for h in range(parts):
        width = column_refs[h].shape[1]
        piece = lax.dot_general(
            deficit_ref[:, span(place_of(parts, pos_ref[0], h) * width, width)],
            column_refs[h][...],
            (((1,), (1,)), ((), ())),
            preferred_element_type=f32,
        )
        total = piece if total is None else total + piece
    out_ref[...] = total


def far_kernel(cluster_ref, own_cluster_ref, basis_ref, out_ref):
    rows, slots, rank, panel = basis_ref.shape
    clusters = out_ref.shape[0] // rank
    for r in range(rows):
        for j in range(clusters):
            wanted = own_cluster_ref[0] ^ j
            block = jnp.zeros((rank, panel), f32)
            for k in range(slots):
                live = cluster_ref[r, k] == wanted
                block = jnp.where(live, basis_ref[r, k].astype(f32), block)
            out_ref[j * rank : (j + 1) * rank, r * panel : (r + 1) * panel] = block.astype(bf16)


def near_kernel(own_panels, total_panels, column_ref, count_ref, pos_ref, own_ref, near_ref, far_ref, blocks_ref, out_ref, window):
    rows, slots = column_ref.shape
    members = own_ref.shape[0]
    odd = pos_ref[0] % 2
    for side, start in ((own_ref, own_panels), (near_ref, (1 - odd) * 2 * own_panels), (far_ref, odd * 2 * own_panels)):
        for j in range(own_panels):
            window[start + j] = side[:, j * PANEL : (j + 1) * PANEL].astype(f32)
    window[3 * own_panels] = jnp.zeros((members, PANEL), f32)
    base = (pos_ref[0] - 1) * own_panels
    for r in range(rows):
        total = None
        for s0 in range(0, slots, 4):
            tiles = []
            for s in range(s0, min(s0 + 4, slots)):
                place = lax.rem(column_ref[r, s] - base + total_panels, total_panels)
                tiles.append(window[jnp.where(s < count_ref[r], place, 3 * own_panels)])
            piece = jnp.dot(
                jnp.concatenate(tiles, axis=1).astype(bf16),
                blocks_ref[r, s0 : s0 + 4].reshape(len(tiles) * PANEL, PANEL),
                preferred_element_type=f32,
            )
            total = piece if total is None else total + piece
        out_ref[:, r * PANEL : (r + 1) * PANEL] = total


def last_kernel(parts, pos_ref, low_ref, high_ref, *refs):
    far_refs, near_refs = refs[:parts], refs[parts : 2 * parts]
    base_ref, scale_ref, out_ref = refs[2 * parts :]
    depth = low_ref.shape[1]
    for h in range(parts):
        width = near_refs[h].shape[1]
        lanes = span(place_of(parts, pos_ref[0], h) * width, width)
        stress = (
            near_refs[h][...]
            + jnp.dot(low_ref[...], far_refs[h][:depth], preferred_element_type=f32)
            + jnp.dot(high_ref[...], far_refs[h][depth:], preferred_element_type=f32)
        )
        out_ref[:, lanes] = base_ref[:, lanes] + scale_ref[:, lanes] * stress


def per_device(
    log_rate,
    log_state,
    direct_effect,
    evolution_effect,
    slip_distance,
    normal_stress,
    near_blocks,
    near_columns,
    near_count,
    far_clusters,
    far_basis,
    column_basis,
):
    fault_count = lax.axis_size("fault")
    parts = lax.axis_size("member")
    fault_pos = lax.axis_index("fault")
    member_pos = lax.axis_index("member")
    local_members, elements = log_rate.shape
    own_panels = elements // PANEL
    total_panels = own_panels * fault_count
    row_count, slots = near_columns.shape
    row_width = row_count * PANEL
    rank_size = column_basis.shape[0]
    cluster_total = fault_count // GROUP
    members = parts * local_members
    def gathered(block):
        if parts == 2:
            return [block, swapped(block, "member", lambda i: i ^ 1)]
        every = lax.all_gather(block, "member", axis=0)
        return [every[h] for h in range(parts)]

    def call(body, name, out_shape, specs, mib=2, flops=10**6, scratch=()):
        return pl.pallas_call(
            body,
            out_shape=[jax.ShapeDtypeStruct(*o) for o in out_shape],
            in_specs=specs,
            out_specs=[IN_VMEM] * len(out_shape),
            scratch_shapes=scratch,
            compiler_params=pltpu.CompilerParams(vmem_limit_bytes=mib << 20),
            cost_estimate=pl.CostEstimate(flops=flops, bytes_accessed=1, transcendentals=0),
            name=name,
        )

    if parts == 2:
        other = swapped(in_hbm(column_basis), "member", lambda i: i ^ 1)
        columns = [column_basis, pltpu.with_memory_space_constraint(other, pltpu.VMEM)]
    else:
        columns = gathered(column_basis)
    (far_by_cluster,) = call(
        far_kernel,
        "far_by_cluster",
        [((cluster_total * rank_size, row_width), bf16)],
        [IN_SMEM, IN_SMEM, IN_VMEM],
        flops=COST,
    )(in_hbm(far_clusters), (fault_pos // GROUP)[None], in_hbm(far_basis))
    far_all = gathered(far_by_cluster)
    log_rate_later, far_by_cluster = lax.optimization_barrier((log_rate, far_by_cluster))
    (deficit,) = call(
        deficit_kernel, "deficit", [((local_members, elements), bf16)], [IN_VMEM], flops=COST
    )(log_rate_later)
    deficit_all = jnp.concatenate(gathered(deficit), axis=0)
    (partial_value,) = call(
        functools.partial(partial_kernel, parts),
        "partial",
        [((local_members, rank_size), f32)],
        [IN_SMEM] + [IN_VMEM] * (1 + parts),
        flops=COST,
    )(member_pos[None], deficit, *columns)

    total = partial_value + swapped(partial_value, "fault", lambda i: i ^ 1)
    near_side = swapped(deficit_all, "fault", lambda i: i ^ 1)
    far_side = swapped(deficit_all, "fault", lambda i: i + 1 if i % 2 else i - 1)
    bit = 2
    while bit < GROUP:
        total = total + swapped(total, "fault", lambda i: i ^ bit ^ 1)
        bit *= 2
    low = total.astype(bf16)

    (near_field,) = call(
        functools.partial(near_kernel, own_panels, total_panels),
        "near",
        [((members, row_width), f32)],
        [IN_SMEM] * 3 + [IN_VMEM] * 4,
        mib=8,
        flops=COST,
        scratch=[pltpu.VMEM((3 * own_panels + 1, members, PANEL), f32)],
    )(near_columns, near_count, fault_pos[None], deficit_all, near_side, far_side, near_blocks)

    high = None
    while bit < fault_count:
        if high is not None:
            low = jnp.concatenate([low, high], axis=1)
        if 2 * bit == fault_count:
            low, near_field = lax.optimization_barrier((low, near_field))
        high = swapped(low, "fault", lambda i: i ^ bit ^ 1)
        bit *= 2

    near_field = near_field.reshape(parts, local_members, row_width)
    if parts == 2:
        near_rows = [near_field[0], swapped(near_field[1], "member", lambda i: i ^ 1)]
    else:
        exchanged = lax.all_to_all(near_field, "member", 0, 0)
        near_rows = [exchanged[h] for h in range(parts)]

    velocity = jnp.exp(log_rate)
    state_rate = (jnp.exp(-log_state) - velocity) / slip_distance
    resistance = normal_stress[None, :] * direct_effect + damping * velocity
    scale = time_step / resistance
    base = log_rate - scale * (normal_stress[None, :] * evolution_effect * state_rate)
    state_next = log_state + time_step * state_rate
    (rate_next,) = call(
        functools.partial(last_kernel, parts),
        "last",
        [((local_members, elements), f32)],
        [IN_SMEM] + [IN_VMEM] * (4 + 2 * parts),
        flops=COST,
    )(member_pos[None], low, high, *far_all, *near_rows, base, scale)
    return rate_next, state_next


def solution(mesh):
    return jax.shard_map(
        per_device,
        mesh=mesh,
        in_specs=(
            P("member", "fault"),
            P("member", "fault"),
            P("member", "fault"),
            P("member", "fault"),
            P("member", "fault"),
            P("fault"),
            P(("fault", "member"), None, None, None),
            P(("fault", "member"), None),
            P(("fault", "member")),
            P(("fault", "member"), None),
            P(("fault", "member"), None, None, None),
            P(None, ("fault", "member")),
        ),
        out_specs=(P("member", "fault"), P("member", "fault")),
        check_vma=False,
    )
```
